256 devices in a mesh: ep: 32 (over z, y), tp: 8 (over x, core).
Axes of the slice: x: 4, y: 4, z: 8, core: 2. Of those that a mesh axis runs over, the one named last changes fastest.
Arguments:
- tokens: bfloat16 [1024, 6144], P('ep', 'tp'), may hold values from -6 to 6
- expert_ids: int32 [1024, 2], P('ep'), may hold values from 0 to 7, all different within a row; in each aligned block of 32 rows (0 to 31, 32 to 63, ...) at most 16 rows name the same one
- combine_weights: float32 [1024, 2], P('ep'), may hold values from 0.1 to 1
- gate_codes: bfloat16 [6144, 65536], P(None, ('ep', 'tp')), may hold values from -6 to 6, as said below
- gate_scales: bfloat16 [192, 65536], P(None, ('ep', 'tp')), as said below
- up_codes: bfloat16 [6144, 65536], P(None, ('ep', 'tp')), may hold values from -6 to 6, as said below
- up_scales: bfloat16 [192, 65536], P(None, ('ep', 'tp')), as said below
- down_codes: bfloat16 [65536, 6144], P(('ep', 'tp')), may hold values from -6 to 6, as said below
- down_scales: bfloat16 [2048, 6144], P(('ep', 'tp')), as said below
Outputs:
- mixed: bfloat16 [1024, 6144], P('ep', 'tp')
The draws below stay inside these ranges and needn't reach their ends.
Inputs may be any that keep to these rules, and one draw needn't show every extreme that they name: `expert_ids`: each token names 2 different experts. Among the 32 tokens of one index of ep no expert is named more than 16 times, a bound that some block reaches. `gate_codes`: every entry is one of 0, 0.5, 1, 1.5, 2, 3, 4, 6 or its negative. `up_codes`: every entry is one of 0, 0.5, 1, 1.5, 2, 3, 4, 6 or its negative. `down_codes`: every entry is one of 0, 0.5, 1, 1.5, 2, 3, 4, 6 or its negative. `gate_scales`: every entry is a power of two. `up_scales`: every entry is a power of two. `down_scales`: every entry is a power of two.
All inputs are finite; a program needn't handle non-finite values.
Results may differ from the reference program's by a relative error of at most 0.014.
Values may be sent and summed in bfloat16 or wider, within the bound.
A program may use at most 128 MiB of HBM per device.

```python
import math
import jax
import jax.numpy as jnp
import numpy as np
from jax import lax

D = 6144
FF = 8192
EXPERTS = 8
TOPK = 2
TOK_DEV = 32
CAP = 16
FF_DEV = 256
TOKENS = 1024
N_EP = 32


code_levels = (0.0, 0.5, 1.0, 1.5, 2.0, 3.0, 4.0, 6.0, 0.0, -0.5, -1.0, -1.5, -2.0, -3.0, -4.0, -6.0)


def draw_levels(key, salt, count_rows, count_cols):
    picked = jax.random.randint(jax.random.fold_in(key, salt), (count_rows, count_cols), 0, 16)
    table = jnp.array(code_levels, jnp.float32)
    return table[picked].astype(jnp.bfloat16)


def draw_powers(key, salt, count_rows, count_cols):
    powers = jax.random.randint(jax.random.fold_in(key, salt), (count_rows, count_cols), -9, -6)
    return jnp.exp2(powers.astype(jnp.float32)).astype(jnp.bfloat16)


def draw_gate_codes(key, part):
    return draw_levels(key, 11, D, EXPERTS * FF)


def draw_up_codes(key, part):
    return draw_levels(key, 12, D, EXPERTS * FF)


def draw_down_codes(key, part):
    return draw_levels(key, 13, EXPERTS * FF, D)


def draw_gate_scales(key, part):
    return draw_powers(key, 21, D // 32, EXPERTS * FF)


def draw_up_scales(key, part):
    return draw_powers(key, 22, D // 32, EXPERTS * FF)


def draw_down_scales(key, part):
    return draw_powers(key, 23, EXPERTS * FF // 32, D)


def shard_levels(stream_key, dims, cuts, low, high):
    def one(dim, blocks):
        heights = jax.random.uniform(jax.random.fold_in(jax.random.fold_in(stream_key, 6), dim), (blocks,), jnp.float32, low / len(cuts), high / len(cuts))
        return jnp.repeat(jnp.exp(heights), dims[dim] // blocks).reshape((-1,) + (1,) * (len(dims) - dim - 1))

    loudness = one(*cuts[0])
    for cut in cuts[1:]:
        loudness = loudness * one(*cut)
    return loudness


def assign_block(rng, own, number, rows, amount, top, limit, slope):
    ranking = jax.random.permutation(rng, amount)
    crowded, ordinary = portions_of(amount, rows * top, limit, slope, True), portions_of(amount, rows * top, limit, slope, False)
    places = jnp.arange(amount)

    def named(sizes, turn):
        used = int((sizes > 0).sum())
        fixed = max(1, used // 4)
        passed = fixed + (places - fixed + turn * (used - fixed)) % max(1, amount - fixed)
        return jnp.zeros((amount,), jnp.int32).at[ranking[jnp.where(places < fixed, places, passed)]].set(jnp.asarray(sizes, jnp.int32))

    sizes = jnp.where(number % 4 == 0, named(crowded, number // 4), named(ordinary, number - number // 4 - 1))
    mixed = jax.random.permutation(jax.random.fold_in(own, 3), amount)
    giver, receiver = mixed[0:amount // 2 * 2:2], mixed[1:amount // 2 * 2:2]
    room = jnp.minimum(sizes[giver] - 1, limit - sizes[receiver]) // 2
    room = jnp.where((giver == ranking[0]) | (receiver == ranking[0]) | (sizes[receiver] == 0), 0, jnp.maximum(room, 0))
    passed = jax.random.randint(jax.random.fold_in(own, 4), (amount // 2,), 0, 1 << 20) % (room + 1)
    sizes = sizes.at[giver].add(-passed).at[receiver].add(passed)
    members = jnp.searchsorted(jnp.cumsum(sizes), jnp.arange(rows * top), side="right").astype(jnp.int32)
    grid = members.reshape(top, rows).T
    grid = grid[jax.random.permutation(jax.random.fold_in(own, 1), rows)]
    turn = jax.random.randint(jax.random.fold_in(own, 2), (rows, 1), 0, top)
    return jnp.take_along_axis(grid, (jnp.arange(top)[None, :] + turn) % top, axis=1)


def portions_of(amount, total, most, lean, full):
    loads = [(1 << 20) // math.isqrt(grade ** lean) + 1 for grade in range(1, amount + 1)]
    largest = most if full else min(most, max(-(-total // amount), total * loads[0] // sum(loads)))
    least = 1 if total - largest >= amount - 1 else 0
    holding, spare = [largest] + [least] * (amount - 1), total - largest - least * (amount - 1)
    while spare > 0:
        free = [i for i in range(1, amount) if holding[i] < largest] or [i for i in range(1, amount) if holding[i] < most]
        whole, remaining = sum([loads[i] for i in free]), spare
        for i in free:
            more = min(most - holding[i], max(1, remaining * loads[i] // whole), spare)
            holding[i] = holding[i] + more
            spare = spare - more
    return np.array(holding)


def centred(own_key, extent, deviation, bound, cuts=(), kind=jnp.bfloat16):
    values = jax.random.normal(own_key, extent, jnp.float32) * deviation
    if len(cuts) > 0:
        values = shard_levels(own_key, extent, cuts, -0.22, 0.18) * values
    return jnp.clip(values, min=-bound, max=bound).astype(kind)


def setup_inputs(seed: int = 0) -> dict:
    splits = jax.random.split(jax.random.key(seed), 10)
    tokens = centred(splits[0], (TOKENS, D), 1.0, 6.0, ((0, 32), (1, 8)))
    expert_ids_keys = jax.random.split(jax.random.fold_in(splits[1], 1), TOKENS // TOK_DEV)
    expert_ids_turns = jax.random.permutation(jax.random.fold_in(splits[1], 3), TOKENS // TOK_DEV)
    expert_ids = jax.vmap(lambda own, number: assign_block(jax.random.fold_in(splits[1], 2), own, number, TOK_DEV, EXPERTS, TOPK, CAP, 2))(expert_ids_keys, expert_ids_turns).reshape((TOKENS, TOPK))
    combine_weights = jnp.clip(0.1 + 0.9 * jax.random.uniform(splits[2], (TOKENS, TOPK), jnp.float32) ** shard_levels(splits[2], (TOKENS, TOPK), ((0, 32),), -0.2, 0.2), 0.1, 1.0)
    gate_codes = draw_gate_codes(jax.random.fold_in(splits[9], 71), 0)
    gate_scales = draw_gate_scales(jax.random.fold_in(splits[9], 71), 0)
    up_codes = draw_up_codes(jax.random.fold_in(splits[9], 71), 0)
    up_scales = draw_up_scales(jax.random.fold_in(splits[9], 71), 0)
    down_codes = draw_down_codes(jax.random.fold_in(splits[9], 71), 0)
    down_scales = draw_down_scales(jax.random.fold_in(splits[9], 71), 0)
    return {"tokens": tokens, "expert_ids": expert_ids, "combine_weights": combine_weights, "gate_codes": gate_codes, "gate_scales": gate_scales, "up_codes": up_codes, "up_scales": up_scales, "down_codes": down_codes, "down_scales": down_scales}


def dequant(code_values, scales):
    count_in, count_out = code_values.shape
    blocks = code_values.reshape(count_in // 32, 32, count_out) * scales[:, None, :]
    return blocks.reshape(count_in, count_out)


def reference(tokens, expert_ids, combine_weights, gate_codes, gate_scales, up_codes, up_scales, down_codes, down_scales):
    slot_total = N_EP * CAP
    block_ids = expert_ids.reshape(N_EP, TOK_DEV * TOPK)
    is_expert = (block_ids[:, :, None] == jnp.arange(EXPERTS, dtype=jnp.int32)[None, None, :]).astype(jnp.int32)
    before = jnp.cumsum(is_expert, axis=1) - is_expert
    slot_rank = jnp.sum(before * is_expert, axis=2)
    source = jnp.arange(N_EP, dtype=jnp.int32)[:, None]
    global_slot = (source * CAP + slot_rank).reshape(TOKENS, TOPK).astype(jnp.int32)
    slot_index = jnp.arange(slot_total, dtype=jnp.int32)

    def per_expert(mixed_sum, expert):
        keys = jnp.where(expert_ids == expert, global_slot, -1)
        chosen = jnp.zeros((slot_total, TOKENS), jnp.float32)
        weighting = jnp.zeros((TOKENS, slot_total), jnp.float32)
        for column in range(TOPK):
            match_rows = keys[:, column][None, :] == slot_index[:, None]
            chosen = chosen + match_rows.astype(jnp.float32)
            weighting = weighting + combine_weights[:, column][:, None] * jnp.transpose(match_rows).astype(jnp.float32)
        slot_rows = jnp.dot(chosen.astype(jnp.bfloat16), tokens, preferred_element_type=jnp.float32).astype(jnp.bfloat16)
        start = (expert * FF).astype(jnp.int32)
        start_block = (expert * (FF // 32)).astype(jnp.int32)
        gate_matrix = dequant(lax.dynamic_slice_in_dim(gate_codes, start, FF, 1), lax.dynamic_slice_in_dim(gate_scales, start, FF, 1))
        up_matrix = dequant(lax.dynamic_slice_in_dim(up_codes, start, FF, 1), lax.dynamic_slice_in_dim(up_scales, start, FF, 1))
        down_matrix = dequant(lax.dynamic_slice_in_dim(down_codes, start, FF, 0), lax.dynamic_slice_in_dim(down_scales, start_block, FF // 32, 0))
        gate_proj = jnp.dot(slot_rows, gate_matrix, preferred_element_type=jnp.float32)
        up_proj = jnp.dot(slot_rows, up_matrix, preferred_element_type=jnp.float32)
        hidden = (jax.nn.silu(gate_proj) * up_proj).astype(jnp.bfloat16)

        def add_block(total, block):
            lower = (block * FF_DEV).astype(jnp.int32)
            piece = lax.dynamic_slice_in_dim(hidden, lower, FF_DEV, 1)
            block_weights = lax.dynamic_slice_in_dim(down_matrix, lower, FF_DEV, 0)
            rounded = lax.optimization_barrier(jnp.dot(piece, block_weights, preferred_element_type=jnp.float32).astype(jnp.bfloat16))
            return total + rounded.astype(jnp.float32), None

        expert_out, _ = lax.scan(add_block, jnp.zeros((slot_total, D), jnp.float32), jnp.arange(FF // FF_DEV, dtype=jnp.int32))
        added = jnp.dot(weighting, expert_out, precision=lax.Precision.HIGHEST, preferred_element_type=jnp.float32)
        return mixed_sum + added, None

    mixed_sum, _ = lax.scan(per_expert, jnp.zeros((TOKENS, D), jnp.float32), jnp.arange(EXPERTS, dtype=jnp.int32))
    return mixed_sum.astype(jnp.bfloat16)
```

```python
import functools

import jax
import jax.numpy as jnp
from jax import lax
from jax.experimental import pallas as pl
from jax.experimental.pallas import tpu as pltpu
from jax.sharding import PartitionSpec as P

EXPERTS = 8
CAP = 16
NX, NY, NZ = 4, 4, 8
MESH = pl.DeviceIdType.MESH
BF, F32 = jnp.bfloat16, jnp.float32


def mult(value, factor):
    return pl.multiple_of(value, factor)


def kernel(
    tokens, ids, combine, gate_c, gate_s, up_c, up_s, down_c, down_s,
    out,
    packed, X, PS, H, FIN, YB, WMAT, RA, RB, RA2, RB2,
    GC, GS, UC, US, DC, DS,
    wl_sem, ws_sem, wr_sem, zs_sem, zr_sem, zl_sem,
    as_sem, ar_sem, bs_sem, br_sem,
    rs_send, rs_recv, fs_sem, fr_sem,
):
    ep, tp = lax.axis_index("ep"), lax.axis_index("tp")
    z, y = ep // NY, lax.rem(ep, NY)
    x, c = tp // 2, lax.rem(tp, 2)
    feat = tokens.shape[1]
    wide = 2 * feat
    parity = lax.rem(z, 2)
    xs = [lax.rem(x + d, NX) for d in range(NX)]
    ys = [lax.rem(y + d, NY) for d in range(NY)]

    def dev(zz, yy, xx, cc):
        return (zz * NY + yy, xx * 2 + cc)

    dev_x = {1: dev(z, y, xs[1], c), -1: dev(z, y, xs[3], c)}
    dev_y = {1: dev(z, ys[1], x, c), -1: dev(z, ys[3], x, c)}
    partner = dev(z, y, x, 1 - c)

    barrier = pltpu.get_barrier_semaphore()
    greeted = [partner, dev_x[1], dev_x[-1], dev_y[1], dev_y[-1]]
    for dz in range(1, NZ):
        zt = lax.rem(z + dz, NZ)
        greeted += [dev(zt, y, x, c), dev(zt, y, x, 1 - c)]
    for who in greeted:
        pl.semaphore_signal(barrier, inc=1, device_id=who, device_id_type=MESH)

    weights = [(gate_c, GC), (gate_s, GS), (up_c, UC), (up_s, US), (down_c, DC), (down_s, DS)]
    local_w = []
    for i, (src, dst) in enumerate(weights):
        copy = pltpu.make_async_copy(src, dst.at[0], wl_sem.at[i])
        copy.start()
        local_w.append(copy)

    count = ids.shape[1]
    slot = lax.broadcasted_iota(jnp.int32, (EXPERTS * CAP, count), 0)
    expert, rank = slot // CAP, lax.rem(slot, CAP)
    first = ids[0:1, :] == expert
    second = ids[1:2, :] == expert
    member = jnp.logical_or(first, second)
    before = (
        lax.broadcasted_iota(jnp.int32, (count, count), 0)
        < lax.broadcasted_iota(jnp.int32, (count, count), 1)
    )
    member_rank = jnp.dot(
        member.astype(F32).astype(BF), before.astype(F32).astype(BF), preferred_element_type=F32
    )
    chosen = jnp.logical_and(member, member_rank == rank.astype(F32))
    packed[...] = jnp.dot(
        chosen.astype(F32).astype(BF), tokens[...], preferred_element_type=F32
    ).astype(BF)
    WMAT[...] = jnp.where(
        chosen, jnp.where(first, combine[0:1, :], combine[1:2, :]), 0.0
    )

    pl.semaphore_wait(barrier, len(greeted))

    z_row = mult(y * 64 + (z // 2) * 16, 16)
    z_col = mult(x * wide + c * feat, 128)
    z_idx = (z // 2) * 2 + c
    at_home = c == parity
    z_sends = []
    for dz in (4, 3, 5, 2, 6, 1, 7, 0):
        zt = lax.rem(z + dz, NZ)
        z_sends.append((dz, pltpu.make_async_remote_copy(
            src_ref=packed.at[pl.ds(mult(zt * CAP, CAP), CAP), :],
            dst_ref=X.at[pl.ds(z_row, CAP), pl.ds(z_col, feat)],
            send_sem=zs_sem.at[dz],
            recv_sem=zr_sem.at[z_idx],
            device_id=dev(zt, y, x, parity),
            device_id_type=MESH,
        )))
    for dz, copy in z_sends:
        if dz == 0:
            pl.when(jnp.logical_not(at_home))(copy.start)
        else:
            copy.start()
    remote_w = []
    for i, (src, dst) in enumerate(weights):
        copy = pltpu.make_async_remote_copy(
            src_ref=src, dst_ref=dst.at[1], send_sem=ws_sem.at[i], recv_sem=wr_sem.at[i],
            device_id=partner, device_id_type=MESH,
        )
        copy.start()
        remote_w.append(copy)

    @pl.when(at_home)
    def _():
        copy = pltpu.make_async_copy(
            packed.at[pl.ds(mult(z * CAP, CAP), CAP), :],
            X.at[pl.ds(z_row, CAP), pl.ds(z_col, feat)],
            zl_sem,
        )
        copy.start()
        copy.wait()

    def z_arrived(zi):
        for cc in range(2):
            region = X.at[
                pl.ds(mult(y * 64 + zi * 16, 16), CAP),
                pl.ds(mult(x * wide + cc * feat, 128), feat),
            ]
            copy = pltpu.make_async_remote_copy(
                src_ref=region, dst_ref=region, send_sem=zs_sem.at[0],
                recv_sem=zr_sem.at[zi * 2 + cc], device_id=partner, device_id_type=MESH,
            )
            here = jnp.logical_and(2 * zi + c == z, c == cc)
            pl.when(jnp.logical_not(here))(copy.wait_recv)

    def region(ref, half, yy, xx, part):
        start, size = {None: (0, 32), 0: (0, 16), 1: (16, 16)}[part]
        return ref.at[
            pl.ds(mult(yy * 64 + half * 32 + start, 16), size),
            pl.ds(mult(xx * wide, 128), wide),
        ]

    sends = []
    SIGN = (1, -1)

    class Gather:
        def __init__(self, half, send_sem, recv_sem):
            self.half, self.ss, self.rs = half, send_sem, recv_sem
            self.line = ys if half == 0 else xs
            self.other = xs if half == 0 else ys
            self.dev1 = dev_y if half == 0 else dev_x
            self.dev2 = dev_x if half == 0 else dev_y

        def reg(self, a, b, part):
            p, q = self.line[a % 4], self.other[b % 4]
            yy, xx = (p, q) if self.half == 0 else (q, p)
            return region(X, self.half, yy, xx, part)

        def send(self, a, b, part, device, index):
            r = self.reg(a, b, part)
            copy = pltpu.make_async_remote_copy(
                src_ref=r, dst_ref=r, send_sem=self.ss.at[index], recv_sem=self.rs.at[index],
                device_id=device, device_id_type=MESH,
            )
            copy.start()
            sends.append(copy)

        def arrived(self, a, b, part, index):
            r = self.reg(a, b, part)
            pltpu.make_async_remote_copy(
                src_ref=r, dst_ref=r, send_sem=self.ss.at[index], recv_sem=self.rs.at[index],
                device_id=partner, device_id_type=MESH,
            ).wait_recv()

        def start1(self):
            self.send(0, 0, None, self.dev1[1], 0)
            self.send(0, 0, None, self.dev1[-1], 1)

        OFF = (0, -1, 1, 2)

        def start2(self, j):
            self.send(self.OFF[j], 0, None, self.dev2[1], 4 + 4 * j)
            self.send(self.OFF[j], 0, None, self.dev2[-1], 5 + 4 * j)

        def pass1(self):
            self.arrived(-1, 0, None, 0)
            self.send(-1, 0, 0, self.dev1[1], 2)
            self.arrived(1, 0, None, 1)
            self.send(1, 0, 1, self.dev1[-1], 3)

        def end1(self):
            self.arrived(2, 0, 0, 2)
            self.arrived(2, 0, 1, 3)

        def pass2(self, j):
            a = self.OFF[j]
            self.arrived(a, -1, None, 4 + 4 * j)
            self.send(a, -1, 0, self.dev2[1], 6 + 4 * j)
            self.arrived(a, 1, None, 5 + 4 * j)
            self.send(a, 1, 1, self.dev2[-1], 7 + 4 * j)

        def end2(self, j):
            self.arrived(self.OFF[j], 2, 0, 6 + 4 * j)
            self.arrived(self.OFF[j], 2, 1, 7 + 4 * j)

    A, B = Gather(0, as_sem, ar_sem), Gather(1, bs_sem, br_sem)
    z_arrived(0)
    z_arrived(1)
    A.start1()
    z_arrived(2)
    z_arrived(3)
    B.start1()
    A.start2(0)
    B.start2(0)
    for g in (A, B):
        g.pass1()
    for g in (A, B):
        g.start2(1)
        g.start2(2)
    for g in (A, B):
        g.pass2(0)
    for g in (A, B):
        g.end1()
        g.start2(3)
    for j in (1, 2, 3):
        for g in (A, B):
            g.pass2(j)
    for j in range(4):
        for g in (A, B):
            g.end2(j)

    for copy in local_w:
        copy.wait()
    for copy in remote_w:
        copy.wait_recv()

    def scaled(codes, scales):
        rows, cols = codes.shape
        blocks = codes.reshape(rows // 32, 32, cols) * scales[:, None, :]
        return blocks.reshape(rows, cols)

    deep = X.shape[1]
    step = 1536
    for s in range(2):
        gate = up = None
        for k in range(deep // step):
            rows, srows = slice(k * step, (k + 1) * step), slice(k * step // 32, (k + 1) * step // 32)
            xk = X[:, rows]
            g = jnp.dot(xk, scaled(GC[s, rows, :], GS[s, srows, :]), preferred_element_type=F32)
            u = jnp.dot(xk, scaled(UC[s, rows, :], US[s, srows, :]), preferred_element_type=F32)
            gate, up = (g, u) if gate is None else (gate + g, up + u)
        hidden = gate / (1.0 + jnp.exp(-gate)) * up
        H[:, s * 256:(s + 1) * 256] = hidden.astype(BF)

    def project(xx):
        piece = 512
        for i in range(wide // piece):
            cols = pl.ds(mult(xx * wide + i * piece, 128), piece)
            total = None
            for s in range(2):
                part = jnp.dot(
                    H[:, s * 256:(s + 1) * 256], scaled(DC[s, :, cols], DS[s, :, cols]),
                    preferred_element_type=F32,
                )
                total = part if total is None else total + part
            PS[:, cols] = total.astype(BF)

    class Reduce:
        def __init__(self, half, base, R1, R2):
            self.half, self.base, self.R1, self.R2 = half, base, R1, R2
            self.line = xs if half == 0 else ys
            self.other = ys if half == 0 else xs
            self.dev1 = dev_x if half == 0 else dev_y
            self.dev2 = dev_y if half == 0 else dev_x

        def reg(self, a, b, part):
            p, q = self.line[a % 4], self.other[b % 4]
            yy, xx = (q, p) if self.half == 0 else (p, q)
            return region(PS, self.half, yy, xx, part)

        def copy(self, src, dst, device, index):
            return pltpu.make_async_remote_copy(
                src_ref=src, dst_ref=dst, send_sem=rs_send.at[self.base + index],
                recv_sem=rs_recv.at[self.base + index], device_id=device, device_id_type=MESH,
            )

        def send(self, src, dst, device, index):
            copy = self.copy(src, dst, device, index)
            copy.start()
            sends.append(copy)

        def arrived(self, dst, index):
            self.copy(dst, dst, partner, index).wait_recv()

        def far(self, pieces, buf, dev_, index):
            self.send(pieces(2, 0), buf.at[pl.ds(64, 16)], dev_[-1], index)
            self.send(pieces(2, 1), buf.at[pl.ds(80, 16)], dev_[1], index + 1)

        def near(self, pieces, buf, dev_, index):
            self.arrived(buf.at[pl.ds(64, 16)], index)
            low = pieces(-1, 0)
            low[...] = (low[...].astype(F32) + buf[64:80, :].astype(F32)).astype(BF)
            self.send(pieces(-1, None), buf.at[pl.ds(32, 32)], dev_[-1], index + 2)
            self.arrived(buf.at[pl.ds(80, 16)], index + 1)
            high = pieces(1, 1)
            high[...] = (high[...].astype(F32) + buf[80:96, :].astype(F32)).astype(BF)
            self.send(pieces(1, None), buf.at[pl.ds(0, 32)], dev_[1], index + 3)

        def own(self, pieces, buf, index):
            self.arrived(buf.at[pl.ds(32, 32)], index + 2)
            self.arrived(buf.at[pl.ds(0, 32)], index + 3)
            total = pieces(0, None)[...].astype(F32) + buf[0:32, :].astype(F32)
            return (total + buf[32:64, :].astype(F32)).astype(BF)

        OFF = (2, 1, -1, 0)

        def ring1(self, j):
            return (lambda a, part: self.reg(a, self.OFF[j], part)), self.R1.at[j], 4 * j

        def far1(self, j):
            pieces, buf, index = self.ring1(j)
            self.far(pieces, buf, self.dev1, index)

        def near1(self, j):
            pieces, buf, index = self.ring1(j)
            self.near(pieces, buf, self.dev1, index)

        def own1(self, j):
            pieces, buf, index = self.ring1(j)
            value = self.own(pieces, buf, index)
            pieces(0, None)[...] = value

        def ring2(self, a, part):
            return self.reg(0, a, part)

        def far2(self):
            self.far(self.ring2, self.R2, self.dev2, 16)

        def near2(self):
            self.near(self.ring2, self.R2, self.dev2, 16)

        def own2(self):
            FIN[self.half * 32:(self.half + 1) * 32, :] = self.own(self.ring2, self.R2, 16)

    RA_, RB_ = Reduce(0, 0, RA, RA2), Reduce(1, 20, RB, RB2)
    project(xs[2])
    for j in range(4):
        RA_.far1(j)
    RB_.far1(0)
    project(xs[1])
    RB_.far1(1)
    project(xs[3])
    RB_.far1(2)
    project(xs[0])
    RB_.far1(3)
    for j in range(4):
        RA_.near1(j)
        RB_.near1(j)
    for r in (RA_, RB_):
        r.own1(0)
        r.far2()
    for j in (1, 2):
        for r in (RA_, RB_):
            r.own1(j)
    for r in (RA_, RB_):
        r.near2()
    for r in (RA_, RB_):
        r.own1(3)

    returns = []

    def give_back(zi):
        for cc in range(2):
            src = FIN.at[pl.ds(zi * 16, 16), pl.ds(cc * feat, feat)]
            dst = YB.at[pl.ds(mult(z * CAP, CAP), CAP), :]
            copy = pltpu.make_async_remote_copy(
                src_ref=src, dst_ref=dst, send_sem=fs_sem.at[zi * 2 + cc], recv_sem=fr_sem.at[z],
                device_id=dev(2 * zi + c, y, x, cc), device_id_type=MESH,
            )
            here = jnp.logical_and(2 * zi + c == z, c == cc)
            pl.when(jnp.logical_not(here))(copy.start)
            returns.append((here, copy))

            @pl.when(here)
            def _():
                move = pltpu.make_async_copy(src, dst, zl_sem)
                move.start()
                move.wait()

    RA_.own2()
    give_back(0)
    give_back(1)
    RB_.own2()
    give_back(2)
    give_back(3)

    for e in range(EXPERTS):
        dst = YB.at[pl.ds(e * CAP, CAP), :]
        copy = pltpu.make_async_remote_copy(
            src_ref=dst, dst_ref=dst, send_sem=fs_sem.at[0], recv_sem=fr_sem.at[e],
            device_id=partner, device_id_type=MESH,
        )
        here = jnp.logical_and(z == e, at_home)
        pl.when(jnp.logical_not(here))(copy.wait_recv)

    weight = WMAT[...]
    high = weight.astype(BF)
    low = (weight - high.astype(F32)).astype(BF)
    dims = (((0,), (0,)), ((), ()))
    mixed = lax.dot_general(high, YB[...], dims, preferred_element_type=F32)
    mixed = mixed + lax.dot_general(low, YB[...], dims, preferred_element_type=F32)
    out[...] = mixed.astype(BF)

    for copy in remote_w:
        copy.wait_send()
    for dz, copy in z_sends:
        if dz == 0:
            pl.when(jnp.logical_not(at_home))(copy.wait_send)
        else:
            copy.wait_send()
    for copy in sends:
        copy.wait_send()
    for here, copy in returns:
        pl.when(jnp.logical_not(here))(copy.wait_send)


def per_device(tokens, ids, combine, gate_c, gate_s, up_c, up_s, down_c, down_s):
    count, feat = tokens.shape
    deep, units = gate_c.shape
    wide = 2 * feat
    vmem, hbm = pl.BlockSpec(memory_space=pltpu.VMEM), pl.BlockSpec(memory_space=pl.ANY)
    dma = pltpu.SemaphoreType.DMA
    return pl.pallas_call(
        kernel,
        out_shape=jax.ShapeDtypeStruct((count, feat), BF),
        in_specs=[vmem] * 3 + [hbm] * 6,
        out_specs=vmem,
        scratch_shapes=[
            pltpu.VMEM((EXPERTS * CAP, feat), BF),
            pltpu.VMEM((256, deep), BF),
            pltpu.VMEM((256, deep), BF),
            pltpu.VMEM((256, 2 * units), BF),
            pltpu.VMEM((64, wide), BF),
            pltpu.VMEM((EXPERTS * CAP, feat), BF),
            pltpu.VMEM((EXPERTS * CAP, count), F32),
            pltpu.VMEM((4, 96, wide), BF),
            pltpu.VMEM((4, 96, wide), BF),
            pltpu.VMEM((96, wide), BF),
            pltpu.VMEM((96, wide), BF),
            pltpu.VMEM((2,) + gate_c.shape, BF),
            pltpu.VMEM((2,) + gate_s.shape, BF),
            pltpu.VMEM((2,) + up_c.shape, BF),
            pltpu.VMEM((2,) + up_s.shape, BF),
            pltpu.VMEM((2,) + down_c.shape, BF),
            pltpu.VMEM((2,) + down_s.shape, BF),
            dma((6,)), dma((6,)), dma((6,)), dma((8,)), dma((8,)), dma,
            dma((20,)), dma((20,)), dma((20,)), dma((20,)),
            dma((40,)), dma((40,)), dma((8,)), dma((8,)),
        ],
        compiler_params=pltpu.CompilerParams(
            collective_id=0, has_side_effects=True, vmem_limit_bytes=63 * 2**20
        ),
        name="moe",
    )(tokens, jnp.transpose(ids), jnp.transpose(combine), gate_c, gate_s, up_c, up_s, down_c, down_s)


def solution(mesh):
    placed = (
        P("ep", "tp"),
        P("ep", None),
        P("ep", None),
        P(None, ("ep", "tp")),
        P(None, ("ep", "tp")),
        P(None, ("ep", "tp")),
        P(None, ("ep", "tp")),
        P(("ep", "tp"), None),
        P(("ep", "tp"), None),
    )
    return jax.shard_map(
        per_device, mesh=mesh, in_specs=placed, out_specs=P("ep", "tp"), check_vma=False
    )
```

```python
import functools

import jax
import jax.numpy as jnp
from jax import lax
from jax.experimental import pallas as pl
from jax.experimental.pallas import tpu as pltpu
from jax.sharding import PartitionSpec as P

EXPERTS = 8
CAP = 16
NX, NY, NZ = 4, 4, 8
MESH = pl.DeviceIdType.MESH
BF, F32 = jnp.bfloat16, jnp.float32


def mult(value, factor):
    return pl.multiple_of(value, factor)


def kernel(
    tokens_in, ids_in, combine_in, gate_c, gate_s, up_c, up_s, down_c, down_s,
    out,
    tokens, ids, combine, GACC, UACC, packed, X, PS, H, FIN, YB, WMAT, RA, RB, RA2, RB2,
    GC, GS, UC, US, DC, DS,
    in_sem, wl_sem, ws_sem, wr_sem, zs_sem, zr_sem, zl_sem,
    as_sem, ar_sem, bs_sem, br_sem,
    rs_send, rs_recv, fs_sem, fr_sem,
):
    ep, tp = lax.axis_index("ep"), lax.axis_index("tp")
    z, y = ep // NY, lax.rem(ep, NY)
    x, c = tp // 2, lax.rem(tp, 2)
    feat = tokens.shape[1]
    wide = 2 * feat
    parity = lax.rem(z, 2)
    xs = [lax.rem(x + d, NX) for d in range(NX)]
    ys = [lax.rem(y + d, NY) for d in range(NY)]

    def dev(zz, yy, xx, cc):
        return (zz * NY + yy, xx * 2 + cc)

    dev_x = {1: dev(z, y, xs[1], c), -1: dev(z, y, xs[3], c)}
    dev_y = {1: dev(z, ys[1], x, c), -1: dev(z, ys[3], x, c)}
    partner = dev(z, y, x, 1 - c)

    inputs = []
    for i, (src, dst) in enumerate(((ids_in, ids), (tokens_in, tokens), (combine_in, combine))):
        copy = pltpu.make_async_copy(src, dst, in_sem.at[i])
        copy.start()
        inputs.append(copy)

    barrier = pltpu.get_barrier_semaphore()
    greeted = [partner, dev_x[1], dev_x[-1], dev_y[1], dev_y[-1]]
    for dz in range(1, NZ):
        zt = lax.rem(z + dz, NZ)
        greeted += [dev(zt, y, x, c), dev(zt, y, x, 1 - c)]
    for who in greeted:
        pl.semaphore_signal(barrier, inc=1, device_id=who, device_id_type=MESH)

    weights = [(gate_c, GC), (gate_s, GS), (up_c, UC), (up_s, US), (down_c, DC), (down_s, DS)]
    local_w = []
    for i, (src, dst) in enumerate(weights):
        copy = pltpu.make_async_copy(src, dst.at[0], wl_sem.at[i])
        copy.start()
        local_w.append(copy)

    for copy in inputs:
        copy.wait()

    count = ids.shape[1]
    slot = lax.broadcasted_iota(jnp.int32, (EXPERTS * CAP, count), 0)
    expert, rank = slot // CAP, lax.rem(slot, CAP)
    first = ids[0:1, :] == expert
    second = ids[1:2, :] == expert
    member = jnp.logical_or(first, second)
    before = (
        lax.broadcasted_iota(jnp.int32, (count, count), 0)
        < lax.broadcasted_iota(jnp.int32, (count, count), 1)
    )
    member_rank = jnp.dot(
        member.astype(F32).astype(BF), before.astype(F32).astype(BF), preferred_element_type=F32
    )
    chosen = jnp.logical_and(member, member_rank == rank.astype(F32))
    packed[...] = jnp.dot(
        chosen.astype(F32).astype(BF), tokens[...], preferred_element_type=F32
    ).astype(BF)
    WMAT[...] = jnp.where(
        chosen, jnp.where(first, combine[0:1, :], combine[1:2, :]), 0.0
    )

    pl.semaphore_wait(barrier, len(greeted))

    odd = lax.rem(c + z, 2)
    place = {0: 0, 3: 16, 1: 128, 2: 144}
    z_col = mult(x * wide + c * feat, 128)
    at_home = c == parity
    z_sends = []
    for dz in (1, 7, 2, 6, 3, 5, 4, 0):
        zt = lax.rem(z + dz, NZ)
        k = ((NZ - dz) % NZ) // 2
        z_sends.append((dz, pltpu.make_async_remote_copy(
            src_ref=packed.at[pl.ds(mult(zt * CAP, CAP), CAP), :],
            dst_ref=X.at[pl.ds(mult(y * 32 + place[k], 16), CAP), pl.ds(z_col, feat)],
            send_sem=zs_sem.at[dz],
            recv_sem=zr_sem.at[k * 2 + c],
            device_id=dev(zt, y, x, parity),
            device_id_type=MESH,
        )))
    for dz, copy in z_sends:
        if dz == 0:
            pl.when(jnp.logical_not(at_home))(copy.start)
        else:
            copy.start()
    remote_w = []
    for i, (src, dst) in enumerate(weights):
        copy = pltpu.make_async_remote_copy(
            src_ref=src, dst_ref=dst.at[1], send_sem=ws_sem.at[i], recv_sem=wr_sem.at[i],
            device_id=partner, device_id_type=MESH,
        )
        copy.start()
        remote_w.append(copy)

    @pl.when(at_home)
    def _():
        copy = pltpu.make_async_copy(
            packed.at[pl.ds(mult(z * CAP, CAP), CAP), :],
            X.at[pl.ds(mult(y * 32, 16), CAP), pl.ds(z_col, feat)],
            zl_sem,
        )
        copy.start()
        copy.wait()

    def z_arrived(k):
        for cc in range(2):
            area = X.at[
                pl.ds(mult(y * 32 + place[k], 16), CAP),
                pl.ds(mult(x * wide + cc * feat, 128), feat),
            ]
            copy = pltpu.make_async_remote_copy(
                src_ref=area, dst_ref=area, send_sem=zs_sem.at[0],
                recv_sem=zr_sem.at[k * 2 + cc], device_id=partner, device_id_type=MESH,
            )
            if k == 0:
                here = jnp.logical_and(odd == 0, c == cc)
                pl.when(jnp.logical_not(here))(copy.wait_recv)
            else:
                copy.wait_recv()

    def region(ref, half, yy, xx, part):
        start, size = {None: (0, 32), 0: (0, 16), 1: (16, 16)}[part]
        return ref.at[
            pl.ds(mult(half * 128 + yy * 32 + start, 16), size),
            pl.ds(mult(xx * wide, 128), wide),
        ]

    sends = []

    class Gather:
        def __init__(self, half, send_sem, recv_sem):
            self.half, self.ss, self.rs = half, send_sem, recv_sem
            self.line = ys if half == 0 else xs
            self.other = xs if half == 0 else ys
            self.dev1 = dev_y if half == 0 else dev_x
            self.dev2 = dev_x if half == 0 else dev_y

        def reg(self, a, b, part):
            p, q = self.line[a % 4], self.other[b % 4]
            yy, xx = (p, q) if self.half == 0 else (q, p)
            return region(X, self.half, yy, xx, part)

        def send(self, a, b, part, device, index):
            r = self.reg(a, b, part)
            copy = pltpu.make_async_remote_copy(
                src_ref=r, dst_ref=r, send_sem=self.ss.at[index], recv_sem=self.rs.at[index],
                device_id=device, device_id_type=MESH,
            )
            copy.start()
            sends.append(copy)

        def arrived(self, a, b, part, index):
            r = self.reg(a, b, part)
            pltpu.make_async_remote_copy(
                src_ref=r, dst_ref=r, send_sem=self.ss.at[index], recv_sem=self.rs.at[index],
                device_id=partner, device_id_type=MESH,
            ).wait_recv()

        OFF = (0, -1, 1, 2)

        def begin1(self, part):
            self.send(0, 0, part, self.dev1[1], 2 * part)
            self.send(0, 0, part, self.dev1[-1], 2 * part + 1)

        def begin2(self, part):
            self.send(0, 0, part, self.dev2[1], 6 + 2 * part)
            self.send(0, 0, part, self.dev2[-1], 7 + 2 * part)

        def start2(self, j):
            a, base = self.OFF[j], 6 + 6 * j
            self.send(a, 0, 0, self.dev2[1], base)
            self.send(a, 0, 1, self.dev2[-1], base + 3)
            self.send(a, 0, 1, self.dev2[1], base + 2)
            self.send(a, 0, 0, self.dev2[-1], base + 1)

        def pass1(self):
            self.arrived(-1, 0, 0, 0)
            self.send(-1, 0, 0, self.dev1[1], 4)
            self.arrived(1, 0, 1, 3)
            self.send(1, 0, 1, self.dev1[-1], 5)
            self.arrived(-1, 0, 1, 2)
            self.arrived(1, 0, 0, 1)

        def end1(self):
            self.arrived(2, 0, 0, 4)
            self.arrived(2, 0, 1, 5)

        def pass2(self, j):
            a, base = self.OFF[j], 6 + 6 * j
            self.arrived(a, -1, 0, base)
            self.send(a, -1, 0, self.dev2[1], base + 4)
            self.arrived(a, 1, 1, base + 3)
            self.send(a, 1, 1, self.dev2[-1], base + 5)

        def rest2(self, j):
            a, base = self.OFF[j], 6 + 6 * j
            self.arrived(a, -1, 1, base + 2)
            self.arrived(a, 1, 0, base + 1)

        def end2(self, j):
            a, base = self.OFF[j], 6 + 6 * j
            self.arrived(a, 2, 0, base + 4)
            self.arrived(a, 2, 1, base + 5)

    def scaled(codes, scales):
        rows, cols = codes.shape
        blocks = codes.reshape(rows // 32, 32, cols) * scales[:, None, :]
        return blocks.reshape(rows, cols)

    def accumulate(xx, fresh):
        cols = pl.ds(mult(xx * wide, 128), wide)
        scale_rows = pl.ds(mult(xx * (wide // 32), 16), wide // 32)
        for s in range(2):
            for codes, scales, total in ((GC, GS, GACC), (UC, US, UACC)):
                value = jnp.dot(
                    X[:, cols], scaled(codes[s, cols, :], scales[s, scale_rows, :]),
                    preferred_element_type=F32,
                )
                total[s] = value if fresh else total[s] + value

    A, B = Gather(0, as_sem, ar_sem), Gather(1, bs_sem, br_sem)
    for k, part in ((0, 0), (3, 1)):
        z_arrived(k)
        A.begin1(part)
        A.begin2(part)
    for k, part in ((1, 0), (2, 1)):
        z_arrived(k)
        B.begin1(part)
    A.pass1()
    B.begin2(0)
    B.begin2(1)
    A.start2(1)
    B.pass1()
    B.start2(1)
    A.end1()
    A.start2(3)
    A.start2(2)
    B.pass2(0)
    B.start2(2)
    A.pass2(0)
    B.end1()
    B.pass2(1)
    B.start2(3)
    A.pass2(1)
    for copy in local_w:
        copy.wait()
    for copy in remote_w[:4]:
        copy.wait_recv()
    B.rest2(0)
    B.end2(0)
    accumulate(xs[0], True)
    B.pass2(2)
    A.pass2(3)
    A.pass2(2)
    B.pass2(3)
    for j in (0, 1, 3, 2):
        A.rest2(j)
    B.rest2(1)
    B.end2(1)
    accumulate(xs[3], False)
    B.rest2(2)
    B.end2(2)
    accumulate(xs[1], False)
    for j in range(4):
        A.end2(j)
    B.rest2(3)
    B.end2(3)
    accumulate(xs[2], False)
    for copy in remote_w[4:]:
        copy.wait_recv()
    units = GACC.shape[2]
    for s in range(2):
        gate = GACC[s]
        hidden = gate / (1.0 + jnp.exp(-gate)) * UACC[s]
        H[:, s * units:(s + 1) * units] = hidden.astype(BF)

    def project(xx):
        piece = 512
        for i in range(wide // piece):
            cols = pl.ds(mult(xx * wide + i * piece, 128), piece)
            total = None
            for s in range(2):
                part = jnp.dot(
                    H[:, s * 256:(s + 1) * 256], scaled(DC[s, :, cols], DS[s, :, cols]),
                    preferred_element_type=F32,
                )
                total = part if total is None else total + part
            PS[:, cols] = total.astype(BF)

    class Reduce:
        def __init__(self, half, base, R1, R2):
            self.half, self.base, self.R1, self.R2 = half, base, R1, R2
            self.line = xs if half == 0 else ys
            self.other = ys if half == 0 else xs
            self.dev1 = dev_x if half == 0 else dev_y
            self.dev2 = dev_y if half == 0 else dev_x

        def reg(self, a, b, part):
            p, q = self.line[a % 4], self.other[b % 4]
            yy, xx = (q, p) if self.half == 0 else (p, q)
            return region(PS, self.half, yy, xx, part)

        def copy(self, src, dst, device, index):
            return pltpu.make_async_remote_copy(
                src_ref=src, dst_ref=dst, send_sem=rs_send.at[self.base + index],
                recv_sem=rs_recv.at[self.base + index], device_id=device, device_id_type=MESH,
            )

        def send(self, src, dst, device, index):
            copy = self.copy(src, dst, device, index)
            copy.start()
            sends.append(copy)

        def arrived(self, dst, index):
            self.copy(dst, dst, partner, index).wait_recv()

        def far(self, pieces, buf, dev_, index):
            self.send(pieces(2, 0), buf.at[pl.ds(64, 16)], dev_[-1], index)
            self.send(pieces(2, 1), buf.at[pl.ds(80, 16)], dev_[1], index + 1)

        def near(self, pieces, buf, dev_, index):
            self.arrived(buf.at[pl.ds(64, 16)], index)
            low = pieces(-1, 0)
            low[...] = (low[...].astype(F32) + buf[64:80, :].astype(F32)).astype(BF)
            self.send(pieces(-1, None), buf.at[pl.ds(32, 32)], dev_[-1], index + 2)
            self.arrived(buf.at[pl.ds(80, 16)], index + 1)
            high = pieces(1, 1)
            high[...] = (high[...].astype(F32) + buf[80:96, :].astype(F32)).astype(BF)
            self.send(pieces(1, None), buf.at[pl.ds(0, 32)], dev_[1], index + 3)

        def own(self, pieces, buf, index):
            self.arrived(buf.at[pl.ds(32, 32)], index + 2)
            self.arrived(buf.at[pl.ds(0, 32)], index + 3)
            total = pieces(0, None)[...].astype(F32) + buf[0:32, :].astype(F32)
            return (total + buf[32:64, :].astype(F32)).astype(BF)

        OFF = (2, 1, -1, 0)

        def ring1(self, j):
            return (lambda a, part: self.reg(a, self.OFF[j], part)), self.R1.at[j], 4 * j

        def far1(self, j):
            pieces, buf, index = self.ring1(j)
            self.far(pieces, buf, self.dev1, index)

        def near1(self, j):
            pieces, buf, index = self.ring1(j)
            self.near(pieces, buf, self.dev1, index)

        def own1(self, j):
            pieces, buf, index = self.ring1(j)
            value = self.own(pieces, buf, index)
            pieces(0, None)[...] = value

        def ring2(self, a, part):
            return self.reg(0, a, part)

        def far2(self):
            self.far(self.ring2, self.R2, self.dev2, 16)

        def near2(self):
            self.near(self.ring2, self.R2, self.dev2, 16)

        def own2(self):
            FIN[self.half * 32:(self.half + 1) * 32, :] = self.own(self.ring2, self.R2, 16)

    RA_, RB_ = Reduce(0, 0, RA, RA2), Reduce(1, 20, RB, RB2)
    project(xs[2])
    for j in range(4):
        RA_.far1(j)
    RB_.far1(0)
    project(xs[1])
    RB_.far1(1)
    project(xs[3])
    RB_.far1(2)
    project(xs[0])
    RB_.far1(3)
    both = (RB_, RA_)
    for j in range(4):
        for r in both:
            r.near1(j)
    for r in both:
        r.own1(0)
        r.far2()
    for j in (1, 2):
        for r in both:
            r.own1(j)
    for r in both:
        r.near2()
    for r in both:
        r.own1(3)

    returns = []

    def give_back(k):
        zt = lax.rem(z + 2 * k + odd, NZ)
        for cc in range(2):
            src = FIN.at[pl.ds({0: 0, 3: 16, 1: 32, 2: 48}[k], 16), pl.ds(cc * feat, feat)]
            dst = YB.at[pl.ds(mult(z * CAP, CAP), CAP), :]
            copy = pltpu.make_async_remote_copy(
                src_ref=src, dst_ref=dst, send_sem=fs_sem.at[k * 2 + cc], recv_sem=fr_sem.at[z],
                device_id=dev(zt, y, x, cc), device_id_type=MESH,
            )
            if k > 0:
                copy.start()
                returns.append((None, copy))
                continue
            here = jnp.logical_and(odd == 0, c == cc)
            pl.when(jnp.logical_not(here))(copy.start)
            returns.append((here, copy))

            @pl.when(here)
            def _():
                move = pltpu.make_async_copy(src, dst, zl_sem)
                move.start()
                move.wait()

    RB_.own2()
    give_back(2)
    give_back(1)
    RA_.own2()
    give_back(3)
    give_back(0)

    for e in range(EXPERTS):
        dst = YB.at[pl.ds(e * CAP, CAP), :]
        copy = pltpu.make_async_remote_copy(
            src_ref=dst, dst_ref=dst, send_sem=fs_sem.at[0], recv_sem=fr_sem.at[e],
            device_id=partner, device_id_type=MESH,
        )
        here = jnp.logical_and(z == e, at_home)
        pl.when(jnp.logical_not(here))(copy.wait_recv)

    weight = WMAT[...]
    high = weight.astype(BF)
    low = (weight - high.astype(F32)).astype(BF)
    dims = (((0,), (0,)), ((), ()))
    mixed = lax.dot_general(high, YB[...], dims, preferred_element_type=F32)
    mixed = mixed + lax.dot_general(low, YB[...], dims, preferred_element_type=F32)
    out[...] = mixed.astype(BF)

    for copy in remote_w:
        copy.wait_send()
    for dz, copy in z_sends:
        if dz == 0:
            pl.when(jnp.logical_not(at_home))(copy.wait_send)
        else:
            copy.wait_send()
    for copy in sends:
        copy.wait_send()
    for here, copy in returns:
        if here is None:
            copy.wait_send()
        else:
            pl.when(jnp.logical_not(here))(copy.wait_send)


def per_device(tokens, ids, combine, gate_c, gate_s, up_c, up_s, down_c, down_s):
    count, feat = tokens.shape
    deep, units = gate_c.shape
    wide = 2 * feat
    vmem, hbm = pl.BlockSpec(memory_space=pltpu.VMEM), pl.BlockSpec(memory_space=pl.ANY)
    dma = pltpu.SemaphoreType.DMA
    return pl.pallas_call(
        kernel,
        out_shape=jax.ShapeDtypeStruct((count, feat), BF),
        in_specs=[hbm] * 9,
        out_specs=vmem,
        scratch_shapes=[
            pltpu.VMEM((count, feat), BF),
            pltpu.VMEM((2, count), jnp.int32),
            pltpu.VMEM((2, count), F32),
            pltpu.VMEM((2, 256, units), F32),
            pltpu.VMEM((2, 256, units), F32),
            pltpu.VMEM((EXPERTS * CAP, feat), BF),
            pltpu.VMEM((256, deep), BF),
            pltpu.VMEM((256, deep), BF),
            pltpu.VMEM((256, 2 * units), BF),
            pltpu.VMEM((64, wide), BF),
            pltpu.VMEM((EXPERTS * CAP, feat), BF),
            pltpu.VMEM((EXPERTS * CAP, count), F32),
            pltpu.VMEM((4, 96, wide), BF),
            pltpu.VMEM((4, 96, wide), BF),
            pltpu.VMEM((96, wide), BF),
            pltpu.VMEM((96, wide), BF),
            pltpu.VMEM((2,) + gate_c.shape, BF),
            pltpu.VMEM((2,) + gate_s.shape, BF),
            pltpu.VMEM((2,) + up_c.shape, BF),
            pltpu.VMEM((2,) + up_s.shape, BF),
            pltpu.VMEM((2,) + down_c.shape, BF),
            pltpu.VMEM((2,) + down_s.shape, BF),
            dma((3,)), dma((6,)), dma((6,)), dma((6,)), dma((8,)), dma((8,)), dma,
            dma((30,)), dma((30,)), dma((30,)), dma((30,)),
            dma((40,)), dma((40,)), dma((8,)), dma((8,)),
        ],
        compiler_params=pltpu.CompilerParams(
            collective_id=0, has_side_effects=True, vmem_limit_bytes=63 * 2**20
        ),
        name="moe",
    )(tokens, jnp.transpose(ids), jnp.transpose(combine), gate_c, gate_s, up_c, up_s, down_c, down_s)


def solution(mesh):
    placed = (
        P("ep", "tp"),
        P("ep", None),
        P("ep", None),
        P(None, ("ep", "tp")),
        P(None, ("ep", "tp")),
        P(None, ("ep", "tp")),
        P(None, ("ep", "tp")),
        P(("ep", "tp"), None),
        P(("ep", "tp"), None),
    )
    return jax.shard_map(
        per_device, mesh=mesh, in_specs=placed, out_specs=P("ep", "tp"), check_vma=False
    )
```

```python
import functools

import jax
import jax.numpy as jnp
from jax import lax
from jax.experimental import pallas as pl
from jax.experimental.pallas import tpu as pltpu
from jax.sharding import PartitionSpec as P

EXPERTS = 8
CAP = 16
NX, NY, NZ = 4, 4, 8
MESH = pl.DeviceIdType.MESH
BF, F32 = jnp.bfloat16, jnp.float32


GATHER_ORDER = (
    (0, 6), (0, 1), (0, 7), (0, 0), (0, 3), (0, 8), (0, 9), (0, 2), (1, 7), (1, 6),
    (1, 1), (1, 0), (1, 8), (1, 3), (1, 9), (1, 2), (0, 4), (0, 13), (0, 19), (0, 18),
    (0, 12), (0, 5), (0, 21), (1, 13), (1, 12), (1, 15), (1, 18), (1, 4), (1, 5), (1, 14),
    (1, 21), (0, 22), (0, 24), (1, 10), (0, 26), (1, 20), (1, 11), (0, 16), (0, 15), (0, 25),
    (1, 19), (0, 20), (0, 27), (1, 24), (1, 27), (1, 17), (0, 23), (1, 22), (1, 23), (0, 11),
    (0, 17), (1, 16), (1, 26), (0, 14), (1, 25), (0, 10), (2, 0), (1, 29), (1, 28), (0, 29),
    (0, 28), (2, 3), (2, 1), (2, 2),
)
REDUCE_ORDER = (
    (2, 2), (1, 1), (1, 0), (0, 1), (0, 0), (2, 0), (0, 4), (1, 13), (0, 13), (1, 12),
    (2, 1), (0, 5), (0, 8), (1, 5), (1, 4), (2, 3), (1, 9), (1, 8), (0, 9), (1, 3),
    (0, 2), (1, 2), (0, 3), (1, 7), (0, 10), (1, 6), (0, 7), (1, 10), (1, 11), (1, 20),
    (1, 16), (1, 17), (0, 6), (0, 11), (1, 14), (0, 12), (0, 20), (1, 15), (0, 16), (1, 21),
    (0, 17), (1, 19), (1, 22), (1, 18), (0, 15), (0, 22), (0, 21), (0, 14), (0, 18), (1, 23),
    (0, 19), (1, 24), (0, 23), (0, 24),
)


def mult(value, factor):
    return pl.multiple_of(value, factor)


def kernel(
    tokens_in, ids_in, combine_in, gate_c, gate_s, up_c, up_s, down_c, down_s,
    out,
    tokens, ids, combine, GACC, UACC, packed, X, PS, H, FIN, YB, WMAT, RA, RB, RA2, RB2,
    GC, GS, UC, US, DC, DS,
    in_sem, wl_sem, ws_sem, wr_sem, zs_sem, zr_sem, zl_sem,
    as_sem, ar_sem, bs_sem, br_sem,
    rs_send, rs_recv, fs_sem, fr_sem,
):
    ep, tp = lax.axis_index("ep"), lax.axis_index("tp")
    z, y = ep // NY, lax.rem(ep, NY)
    x, c = tp // 2, lax.rem(tp, 2)
    feat = tokens.shape[1]
    wide = 2 * feat
    parity = lax.rem(z, 2)
    xs = [lax.rem(x + d, NX) for d in range(NX)]
    ys = [lax.rem(y + d, NY) for d in range(NY)]

    def dev(zz, yy, xx, cc):
        return (zz * NY + yy, xx * 2 + cc)

    dev_x = {1: dev(z, y, xs[1], c), -1: dev(z, y, xs[3], c)}
    dev_y = {1: dev(z, ys[1], x, c), -1: dev(z, ys[3], x, c)}
    partner = dev(z, y, x, 1 - c)

    inputs = []
    for i, (src, dst) in enumerate(((ids_in, ids), (tokens_in, tokens), (combine_in, combine))):
        copy = pltpu.make_async_copy(src, dst, in_sem.at[i])
        copy.start()
        inputs.append(copy)

    barrier = pltpu.get_barrier_semaphore()
    greeted = [partner, dev_x[1], dev_x[-1], dev_y[1], dev_y[-1]]
    for dz in range(1, NZ):
        zt = lax.rem(z + dz, NZ)
        greeted += [dev(zt, y, x, c), dev(zt, y, x, 1 - c)]
    for who in greeted:
        pl.semaphore_signal(barrier, inc=1, device_id=who, device_id_type=MESH)

    weights = [(gate_c, GC), (gate_s, GS), (up_c, UC), (up_s, US), (down_c, DC), (down_s, DS)]
    local_w = []
    for i, (src, dst) in enumerate(weights):
        copy = pltpu.make_async_copy(src, dst.at[0], wl_sem.at[i])
        copy.start()
        local_w.append(copy)

    for copy in inputs:
        copy.wait()

    count = ids.shape[1]
    slot = lax.broadcasted_iota(jnp.int32, (EXPERTS * CAP, count), 0)
    expert, rank = slot // CAP, lax.rem(slot, CAP)
    first = ids[0:1, :] == expert
    second = ids[1:2, :] == expert
    member = jnp.logical_or(first, second)
    before = (
        lax.broadcasted_iota(jnp.int32, (count, count), 0)
        < lax.broadcasted_iota(jnp.int32, (count, count), 1)
    )
    member_rank = jnp.dot(
        member.astype(F32).astype(BF), before.astype(F32).astype(BF), preferred_element_type=F32
    )
    chosen = jnp.logical_and(member, member_rank == rank.astype(F32))
    packed[...] = jnp.dot(
        chosen.astype(F32).astype(BF), tokens[...], preferred_element_type=F32
    ).astype(BF)
    WMAT[...] = jnp.where(
        chosen, jnp.where(first, combine[0:1, :], combine[1:2, :]), 0.0
    )

    pl.semaphore_wait(barrier, len(greeted))

    odd = lax.rem(c + z, 2)
    place = {0: 0, 3: 16, 1: 128, 2: 144}
    z_col = mult(x * wide + c * feat, 128)
    at_home = c == parity
    z_sends = []
    for dz in (1, 7, 2, 6, 3, 5, 4, 0):
        zt = lax.rem(z + dz, NZ)
        k = ((NZ - dz) % NZ) // 2
        z_sends.append((dz, pltpu.make_async_remote_copy(
            src_ref=packed.at[pl.ds(mult(zt * CAP, CAP), CAP), :],
            dst_ref=X.at[pl.ds(mult(y * 32 + place[k], 16), CAP), pl.ds(z_col, feat)],
            send_sem=zs_sem.at[dz],
            recv_sem=zr_sem.at[k * 2 + c],
            device_id=dev(zt, y, x, parity),
            device_id_type=MESH,
        )))
    for dz, copy in z_sends:
        if dz == 0:
            pl.when(jnp.logical_not(at_home))(copy.start)
        else:
            copy.start()
    remote_w = []
    for i, (src, dst) in enumerate(weights):
        copy = pltpu.make_async_remote_copy(
            src_ref=src, dst_ref=dst.at[1], send_sem=ws_sem.at[i], recv_sem=wr_sem.at[i],
            device_id=partner, device_id_type=MESH,
        )
        copy.start()
        remote_w.append(copy)

    @pl.when(at_home)
    def _():
        copy = pltpu.make_async_copy(
            packed.at[pl.ds(mult(z * CAP, CAP), CAP), :],
            X.at[pl.ds(mult(y * 32, 16), CAP), pl.ds(z_col, feat)],
            zl_sem,
        )
        copy.start()
        copy.wait()

    def z_arrived(k):
        for cc in range(2):
            area = X.at[
                pl.ds(mult(y * 32 + place[k], 16), CAP),
                pl.ds(mult(x * wide + cc * feat, 128), feat),
            ]
            copy = pltpu.make_async_remote_copy(
                src_ref=area, dst_ref=area, send_sem=zs_sem.at[0],
                recv_sem=zr_sem.at[k * 2 + cc], device_id=partner, device_id_type=MESH,
            )
            if k == 0:
                here = jnp.logical_and(odd == 0, c == cc)
                pl.when(jnp.logical_not(here))(copy.wait_recv)
            else:
                copy.wait_recv()

    def region(ref, half, yy, xx, part):
        start, size = {None: (0, 32), 0: (0, 16), 1: (16, 16)}[part]
        return ref.at[
            pl.ds(mult(half * 128 + yy * 32 + start, 16), size),
            pl.ds(mult(xx * wide, 128), wide),
        ]

    sends = []

    class Gather:
        def __init__(self, half, send_sem, recv_sem):
            self.half, self.ss, self.rs = half, send_sem, recv_sem
            self.line = ys if half == 0 else xs
            self.other = xs if half == 0 else ys
            self.dev1 = dev_y if half == 0 else dev_x
            self.dev2 = dev_x if half == 0 else dev_y

        def reg(self, a, b, part):
            p, q = self.line[a % 4], self.other[b % 4]
            yy, xx = (p, q) if self.half == 0 else (q, p)
            return region(X, self.half, yy, xx, part)

        def send(self, a, b, part, device, index):
            r = self.reg(a, b, part)
            copy = pltpu.make_async_remote_copy(
                src_ref=r, dst_ref=r, send_sem=self.ss.at[index], recv_sem=self.rs.at[index],
                device_id=device, device_id_type=MESH,
            )
            copy.start()
            sends.append(copy)

        def arrived(self, a, b, part, index):
            r = self.reg(a, b, part)
            pltpu.make_async_remote_copy(
                src_ref=r, dst_ref=r, send_sem=self.ss.at[index], recv_sem=self.rs.at[index],
                device_id=partner, device_id_type=MESH,
            ).wait_recv()

        OFF = (0, -1, 1, 2)
        CAME = {(-1, 0): 0, (1, 0): 1, (-1, 1): 2, (1, 1): 3, (2, 0): 4, (2, 1): 5}

        def where(self, index):
            ring, i = divmod(index, 6)
            part = i - 4 if i > 3 else i // 2
            step = (2, 2, 0, 1) if i > 3 else ((-1, 0, 1, 1), (1, 0, -1, -1))[i % 2]
            return ring, i, part, step[0]

        def go(self, index):
            ring, i, part, _ = self.where(index)
            up = 1 if i in (0, 2, 4) else -1
            moved = 0 if i < 4 else -up
            if ring == 0:
                a, b, device = moved, 0, self.dev1[up]
            else:
                a, b, device = self.OFF[ring - 1], moved, self.dev2[up]
            if i > 3:
                self.need(index - i + (0 if i == 4 else 3))
            elif ring > 1:
                self.need(self.CAME[(a, part)])
            elif a == 0 and moved == 0:
                self.slots(part)
            self.send(a, b, part, device, index)

        def slots(self, part):
            k = {(0, 0): 0, (0, 1): 3, (1, 0): 1, (1, 1): 2}[(self.half, part)]
            if k not in landed:
                landed.add(k)
                z_arrived(k)

        def need(self, index):
            if (self.half, index) in landed:
                return
            landed.add((self.half, index))
            ring, i, part, off = self.where(index)
            a, b = (off, 0) if ring == 0 else (self.OFF[ring - 1], off)
            self.arrived(a, b, part, index)

    def scaled(codes, scales):
        rows, cols = codes.shape
        blocks = codes.reshape(rows // 32, 32, cols) * scales[:, None, :]
        return blocks.reshape(rows, cols)

    def accumulate(xx, fresh):
        cols = pl.ds(mult(xx * wide, 128), wide)
        scale_rows = pl.ds(mult(xx * (wide // 32), 16), wide // 32)
        for s in range(2):
            for codes, scales, total in ((GC, GS, GACC), (UC, US, UACC)):
                value = jnp.dot(
                    X[:, cols], scaled(codes[s, cols, :], scales[s, scale_rows, :]),
                    preferred_element_type=F32,
                )
                total[s] = value if fresh else total[s] + value

    A, B = Gather(0, as_sem, ar_sem), Gather(1, bs_sem, br_sem)
    halves = (A, B)
    landed = set()
    def column(offset):
        low, high = {0: (None, None), 3: ((0, 2), 1), 1: ((1, 3), 2), 2: ((4, 5), 3)}[offset]
        if offset == 0:
            for i in range(6):
                A.need(i)
            B.slots(0)
            B.slots(1)
        else:
            for j in range(4):
                for i in low:
                    A.need(6 + 6 * j + i)
            for i in low:
                B.need(i)
        for i in range(6):
            B.need(6 + 6 * (high or 0) + i)

    fresh = True
    for kind, index in GATHER_ORDER:
        if kind < 2:
            halves[kind].go(index)
            continue
        if fresh:
            for copy in local_w:
                copy.wait()
            for copy in remote_w[:4]:
                copy.wait_recv()
        column(index)
        accumulate(xs[index], fresh)
        fresh = False
    for half in range(2):
        for index in range(30):
            halves[half].need(index)
    for copy in remote_w[4:]:
        copy.wait_recv()
    units = GACC.shape[2]
    for s in range(2):
        gate = GACC[s]
        hidden = gate / (1.0 + jnp.exp(-gate)) * UACC[s]
        H[:, s * units:(s + 1) * units] = hidden.astype(BF)

    def project(xx):
        piece = 512
        for i in range(wide // piece):
            cols = pl.ds(mult(xx * wide + i * piece, 128), piece)
            total = None
            for s in range(2):
                part = jnp.dot(
                    H[:, s * 256:(s + 1) * 256], scaled(DC[s, :, cols], DS[s, :, cols]),
                    preferred_element_type=F32,
                )
                total = part if total is None else total + part
            PS[:, cols] = total.astype(BF)

    class Reduce:
        def __init__(self, half, base, R1, R2):
            self.half, self.base, self.R1, self.R2 = half, base, R1, R2
            self.line = xs if half == 0 else ys
            self.other = ys if half == 0 else xs
            self.dev1 = dev_x if half == 0 else dev_y
            self.dev2 = dev_y if half == 0 else dev_x

        def reg(self, a, b, part):
            p, q = self.line[a % 4], self.other[b % 4]
            yy, xx = (q, p) if self.half == 0 else (p, q)
            return region(PS, self.half, yy, xx, part)

        def copy(self, src, dst, device, index):
            return pltpu.make_async_remote_copy(
                src_ref=src, dst_ref=dst, send_sem=rs_send.at[self.base + index],
                recv_sem=rs_recv.at[self.base + index], device_id=device, device_id_type=MESH,
            )

        def send(self, src, dst, device, index):
            copy = self.copy(src, dst, device, index)
            copy.start()
            sends.append(copy)

        def arrived(self, dst, index):
            self.copy(dst, dst, partner, index).wait_recv()

        def go(self, index):
            j, i = divmod(index, 4)
            pieces, buf, base = self.ring1(j) if j < 4 else (self.ring2, self.R2, 16)
            devices = self.dev1 if j < 4 else self.dev2
            down, part = i % 2 == 0, i % 2
            device = devices[-1 if down else 1]
            landing = buf.at[pl.ds(64 + 16 * part, 16)]
            if i < 2:
                self.send(pieces(2, part), landing, device, index)
                return
            a = -1 if down else 1
            self.arrived(landing, base + part)
            mine = pieces(a, part)
            mine[...] = (mine[...].astype(F32) + landing[...].astype(F32)).astype(BF)
            self.send(pieces(a, None), buf.at[pl.ds(32 if down else 0, 32)], device, index)

        def own(self, pieces, buf, index):
            self.arrived(buf.at[pl.ds(32, 32)], index + 2)
            self.arrived(buf.at[pl.ds(0, 32)], index + 3)
            total = pieces(0, None)[...].astype(F32) + buf[0:32, :].astype(F32)
            return (total + buf[32:64, :].astype(F32)).astype(BF)

        OFF = (2, 1, -1, 0)

        def ring1(self, j):
            return (lambda a, part: self.reg(a, self.OFF[j], part)), self.R1.at[j], 4 * j

        def own1(self, j):
            pieces, buf, index = self.ring1(j)
            value = self.own(pieces, buf, index)
            pieces(0, None)[...] = value

        def ring2(self, a, part):
            return self.reg(0, a, part)

        def own2(self):
            FIN[self.half * 32:(self.half + 1) * 32, :] = self.own(self.ring2, self.R2, 16)

    reduces = (Reduce(0, 0, RA, RA2), Reduce(1, 20, RB, RB2))

    returns = []

    def give_back(k):
        zt = lax.rem(z + 2 * k + odd, NZ)
        for cc in range(2):
            src = FIN.at[pl.ds({0: 0, 3: 16, 1: 32, 2: 48}[k], 16), pl.ds(cc * feat, feat)]
            dst = YB.at[pl.ds(mult(z * CAP, CAP), CAP), :]
            copy = pltpu.make_async_remote_copy(
                src_ref=src, dst_ref=dst, send_sem=fs_sem.at[k * 2 + cc], recv_sem=fr_sem.at[z],
                device_id=dev(zt, y, x, cc), device_id_type=MESH,
            )
            if k > 0:
                copy.start()
                returns.append((None, copy))
                continue
            here = jnp.logical_and(odd == 0, c == cc)
            pl.when(jnp.logical_not(here))(copy.start)
            returns.append((here, copy))

            @pl.when(here)
            def _():
                move = pltpu.make_async_copy(src, dst, zl_sem)
                move.start()
                move.wait()

    for kind, index in REDUCE_ORDER:
        if kind == 2:
            project(xs[index])
        elif index < 20:
            reduces[kind].go(index)
        elif index < 24:
            reduces[kind].own1(index - 20)
        else:
            reduces[kind].own2()
            for k in ((3, 0), (2, 1))[kind]:
                give_back(k)

    for e in range(EXPERTS):
        dst = YB.at[pl.ds(e * CAP, CAP), :]
        copy = pltpu.make_async_remote_copy(
            src_ref=dst, dst_ref=dst, send_sem=fs_sem.at[0], recv_sem=fr_sem.at[e],
            device_id=partner, device_id_type=MESH,
        )
        here = jnp.logical_and(z == e, at_home)
        pl.when(jnp.logical_not(here))(copy.wait_recv)

    weight = WMAT[...]
    high = weight.astype(BF)
    low = (weight - high.astype(F32)).astype(BF)
    dims = (((0,), (0,)), ((), ()))
    mixed = lax.dot_general(high, YB[...], dims, preferred_element_type=F32)
    mixed = mixed + lax.dot_general(low, YB[...], dims, preferred_element_type=F32)
    out[...] = mixed.astype(BF)

    for copy in remote_w:
        copy.wait_send()
    for dz, copy in z_sends:
        if dz == 0:
            pl.when(jnp.logical_not(at_home))(copy.wait_send)
        else:
            copy.wait_send()
    for copy in sends:
        copy.wait_send()
    for here, copy in returns:
        if here is None:
            copy.wait_send()
        else:
            pl.when(jnp.logical_not(here))(copy.wait_send)


def per_device(tokens, ids, combine, gate_c, gate_s, up_c, up_s, down_c, down_s):
    count, feat = tokens.shape
    deep, units = gate_c.shape
    wide = 2 * feat
    vmem, hbm = pl.BlockSpec(memory_space=pltpu.VMEM), pl.BlockSpec(memory_space=pl.ANY)
    dma = pltpu.SemaphoreType.DMA
    return pl.pallas_call(
        kernel,
        out_shape=jax.ShapeDtypeStruct((count, feat), BF),
        in_specs=[hbm] * 9,
        out_specs=vmem,
        scratch_shapes=[
            pltpu.VMEM((count, feat), BF),
            pltpu.VMEM((2, count), jnp.int32),
            pltpu.VMEM((2, count), F32),
            pltpu.VMEM((2, 256, units), F32),
            pltpu.VMEM((2, 256, units), F32),
            pltpu.VMEM((EXPERTS * CAP, feat), BF),
            pltpu.VMEM((256, deep), BF),
            pltpu.VMEM((256, deep), BF),
            pltpu.VMEM((256, 2 * units), BF),
            pltpu.VMEM((64, wide), BF),
            pltpu.VMEM((EXPERTS * CAP, feat), BF),
            pltpu.VMEM((EXPERTS * CAP, count), F32),
            pltpu.VMEM((4, 96, wide), BF),
            pltpu.VMEM((4, 96, wide), BF),
            pltpu.VMEM((96, wide), BF),
            pltpu.VMEM((96, wide), BF),
            pltpu.VMEM((2,) + gate_c.shape, BF),
            pltpu.VMEM((2,) + gate_s.shape, BF),
            pltpu.VMEM((2,) + up_c.shape, BF),
            pltpu.VMEM((2,) + up_s.shape, BF),
            pltpu.VMEM((2,) + down_c.shape, BF),
            pltpu.VMEM((2,) + down_s.shape, BF),
            dma((3,)), dma((6,)), dma((6,)), dma((6,)), dma((8,)), dma((8,)), dma,
            dma((30,)), dma((30,)), dma((30,)), dma((30,)),
            dma((40,)), dma((40,)), dma((8,)), dma((8,)),
        ],
        compiler_params=pltpu.CompilerParams(
            collective_id=0, has_side_effects=True, vmem_limit_bytes=63 * 2**20
        ),
        name="moe",
    )(tokens, jnp.transpose(ids), jnp.transpose(combine), gate_c, gate_s, up_c, up_s, down_c, down_s)


def solution(mesh):
    placed = (
        P("ep", "tp"),
        P("ep", None),
        P("ep", None),
        P(None, ("ep", "tp")),
        P(None, ("ep", "tp")),
        P(None, ("ep", "tp")),
        P(None, ("ep", "tp")),
        P(("ep", "tp"), None),
        P(("ep", "tp"), None),
    )
    return jax.shard_map(
        per_device, mesh=mesh, in_specs=placed, out_specs=P("ep", "tp"), check_vma=False
    )
```

```python
import functools

import jax
import jax.numpy as jnp
from jax import lax
from jax.experimental import pallas as pl
from jax.experimental.pallas import tpu as pltpu
from jax.sharding import PartitionSpec as P

EXPERTS = 8
CAP = 16
NX, NY, NZ = 4, 4, 8
MESH = pl.DeviceIdType.MESH
BF, F32 = jnp.bfloat16, jnp.float32


GATHER_ORDER = (
    (0, 6), (0, 1), (0, 7), (0, 0), (0, 3), (0, 8), (0, 9), (0, 2), (1, 7), (1, 6),
    (1, 1), (1, 0), (1, 8), (1, 3), (1, 9), (1, 2), (0, 4), (0, 13), (0, 19), (0, 18),
    (0, 12), (0, 5), (0, 21), (1, 13), (1, 12), (1, 15), (1, 18), (1, 4), (1, 5), (1, 14),
    (1, 21), (0, 22), (0, 24), (1, 10), (0, 26), (1, 20), (1, 11), (0, 16), (0, 15), (0, 25),
    (1, 19), (0, 20), (0, 27), (1, 24), (1, 27), (1, 17), (0, 23), (1, 22), (1, 23), (0, 11),
    (0, 17), (1, 16), (1, 26), (0, 14), (1, 25), (0, 10), (2, 0), (1, 29), (1, 28), (0, 29),
    (0, 28), (2, 3), (2, 1), (2, 2),
)
REDUCE_ORDER = (
    (2, 2), (1, 1), (1, 0), (0, 1), (0, 0), (2, 0), (0, 4), (1, 13), (0, 13), (1, 12),
    (2, 1), (0, 5), (0, 8), (1, 5), (1, 4), (2, 3), (1, 9), (1, 8), (0, 9), (1, 3),
    (0, 2), (1, 2), (0, 3), (1, 7), (0, 10), (1, 6), (0, 7), (1, 10), (1, 11), (1, 20),
    (1, 16), (1, 17), (0, 6), (0, 11), (1, 14), (0, 12), (0, 20), (1, 15), (0, 16), (1, 21),
    (0, 17), (1, 19), (1, 22), (1, 18), (0, 15), (0, 22), (0, 21), (0, 14), (0, 18), (1, 23),
    (0, 19), (1, 24), (0, 23), (0, 24),
)


def mult(value, factor):
    return pl.multiple_of(value, factor)


def kernel(
    tokens_in, ids_in, combine_in, gate_c, gate_s, up_c, up_s, down_c, down_s,
    out,
    tokens, ids, combine, GACC, UACC, packed, X, PS, H, FIN, YB, WMAT, WHI, WLO, RA, RB, RA2, RB2,
    GC, GS, UC, US, DC, DS,
    in_sem, wl_sem, ws_sem, wr_sem, zs_sem, zr_sem, zl_sem,
    as_sem, ar_sem, bs_sem, br_sem,
    rs_send, rs_recv, fs_sem, fr_sem,
):
    ep, tp = lax.axis_index("ep"), lax.axis_index("tp")
    z, y = ep // NY, lax.rem(ep, NY)
    x, c = tp // 2, lax.rem(tp, 2)
    feat = tokens.shape[1]
    wide = 2 * feat
    parity = lax.rem(z, 2)
    xs = [lax.rem(x + d, NX) for d in range(NX)]
    ys = [lax.rem(y + d, NY) for d in range(NY)]

    def dev(zz, yy, xx, cc):
        return (zz * NY + yy, xx * 2 + cc)

    dev_x = {1: dev(z, y, xs[1], c), -1: dev(z, y, xs[3], c)}
    dev_y = {1: dev(z, ys[1], x, c), -1: dev(z, ys[3], x, c)}
    partner = dev(z, y, x, 1 - c)

    inputs = []
    for i, (src, dst) in enumerate(((ids_in, ids), (tokens_in, tokens), (combine_in, combine))):
        copy = pltpu.make_async_copy(src, dst, in_sem.at[i])
        copy.start()
        inputs.append(copy)

    barrier = pltpu.get_barrier_semaphore()
    greeted = []
    for dz in (4, 3, 5, 2, 6, 1, 7):
        zt = lax.rem(z + dz, NZ)
        greeted += [dev(zt, y, x, c), dev(zt, y, x, 1 - c)]
    greeted += [dev_x[1], dev_x[-1], dev_y[1], dev_y[-1], partner]
    for who in greeted:
        pl.semaphore_signal(barrier, inc=1, device_id=who, device_id_type=MESH)

    weights = [(gate_c, GC), (gate_s, GS), (up_c, UC), (up_s, US), (down_c, DC), (down_s, DS)]
    local_w = []
    for i, (src, dst) in enumerate(weights):
        copy = pltpu.make_async_copy(src, dst.at[0], wl_sem.at[i])
        copy.start()
        local_w.append(copy)

    for copy in inputs:
        copy.wait()

    count = ids.shape[1]
    slot = lax.broadcasted_iota(jnp.int32, (EXPERTS * CAP, count), 0)
    expert, rank = slot // CAP, lax.rem(slot, CAP)
    first = ids[0:1, :] == expert
    second = ids[1:2, :] == expert
    member = jnp.logical_or(first, second)
    before = (
        lax.broadcasted_iota(jnp.int32, (count, count), 0)
        < lax.broadcasted_iota(jnp.int32, (count, count), 1)
    )
    member_rank = jnp.dot(
        member.astype(F32).astype(BF), before.astype(F32).astype(BF), preferred_element_type=F32
    )
    chosen = jnp.logical_and(member, member_rank == rank.astype(F32))
    packed[...] = jnp.dot(
        chosen.astype(F32).astype(BF), tokens[...], preferred_element_type=F32
    ).astype(BF)
    WMAT[...] = jnp.where(
        chosen, jnp.where(first, combine[0:1, :], combine[1:2, :]), 0.0
    )

    pl.semaphore_wait(barrier, len(greeted))

    odd = lax.rem(c + z, 2)
    place = {0: 0, 3: 16, 1: 128, 2: 144}
    z_col = mult(x * wide + c * feat, 128)
    at_home = c == parity
    z_sends = []
    for dz in (1, 7, 2, 6, 3, 5, 4, 0):
        zt = lax.rem(z + dz, NZ)
        k = ((NZ - dz) % NZ) // 2
        z_sends.append((dz, pltpu.make_async_remote_copy(
            src_ref=packed.at[pl.ds(mult(zt * CAP, CAP), CAP), :],
            dst_ref=X.at[pl.ds(mult(y * 32 + place[k], 16), CAP), pl.ds(z_col, feat)],
            send_sem=zs_sem.at[dz],
            recv_sem=zr_sem.at[k * 2 + c],
            device_id=dev(zt, y, x, parity),
            device_id_type=MESH,
        )))
    for dz, copy in z_sends:
        if dz == 0:
            pl.when(jnp.logical_not(at_home))(copy.start)
        else:
            copy.start()
    remote_w = []
    for i, (src, dst) in enumerate(weights):
        copy = pltpu.make_async_remote_copy(
            src_ref=src, dst_ref=dst.at[1], send_sem=ws_sem.at[i], recv_sem=wr_sem.at[i],
            device_id=partner, device_id_type=MESH,
        )
        copy.start()
        remote_w.append(copy)

    @pl.when(at_home)
    def _():
        copy = pltpu.make_async_copy(
            packed.at[pl.ds(mult(z * CAP, CAP), CAP), :],
            X.at[pl.ds(mult(y * 32, 16), CAP), pl.ds(z_col, feat)],
            zl_sem,
        )
        copy.start()
        copy.wait()

    weight = WMAT[...]
    high = weight.astype(BF)
    low = (weight - high.astype(F32)).astype(BF)
    slots = weight.shape[0]
    eye = (
        lax.broadcasted_iota(jnp.int32, (slots, slots), 0)
        == lax.broadcasted_iota(jnp.int32, (slots, slots), 1)
    ).astype(F32).astype(BF)
    dims = (((0,), (0,)), ((), ()))
    WHI[...] = lax.dot_general(high, eye, dims, preferred_element_type=F32).astype(BF)
    WLO[...] = lax.dot_general(low, eye, dims, preferred_element_type=F32).astype(BF)

    def z_arrived(k):
        for cc in range(2):
            area = X.at[
                pl.ds(mult(y * 32 + place[k], 16), CAP),
                pl.ds(mult(x * wide + cc * feat, 128), feat),
            ]
            copy = pltpu.make_async_remote_copy(
                src_ref=area, dst_ref=area, send_sem=zs_sem.at[0],
                recv_sem=zr_sem.at[k * 2 + cc], device_id=partner, device_id_type=MESH,
            )
            if k == 0:
                here = jnp.logical_and(odd == 0, c == cc)
                pl.when(jnp.logical_not(here))(copy.wait_recv)
            else:
                copy.wait_recv()

    def region(ref, half, yy, xx, part):
        start, size = {None: (0, 32), 0: (0, 16), 1: (16, 16)}[part]
        return ref.at[
            pl.ds(mult(half * 128 + yy * 32 + start, 16), size),
            pl.ds(mult(xx * wide, 128), wide),
        ]

    sends = []

    class Gather:
        def __init__(self, half, send_sem, recv_sem):
            self.half, self.ss, self.rs = half, send_sem, recv_sem
            self.line = ys if half == 0 else xs
            self.other = xs if half == 0 else ys
            self.dev1 = dev_y if half == 0 else dev_x
            self.dev2 = dev_x if half == 0 else dev_y

        def reg(self, a, b, part):
            p, q = self.line[a % 4], self.other[b % 4]
            yy, xx = (p, q) if self.half == 0 else (q, p)
            return region(X, self.half, yy, xx, part)

        def send(self, a, b, part, device, index):
            r = self.reg(a, b, part)
            copy = pltpu.make_async_remote_copy(
                src_ref=r, dst_ref=r, send_sem=self.ss.at[index], recv_sem=self.rs.at[index],
                device_id=device, device_id_type=MESH,
            )
            copy.start()
            sends.append(copy)

        def arrived(self, a, b, part, index):
            r = self.reg(a, b, part)
            pltpu.make_async_remote_copy(
                src_ref=r, dst_ref=r, send_sem=self.ss.at[index], recv_sem=self.rs.at[index],
                device_id=partner, device_id_type=MESH,
            ).wait_recv()

        OFF = (0, -1, 1, 2)
        CAME = {(-1, 0): 0, (1, 0): 1, (-1, 1): 2, (1, 1): 3, (2, 0): 4, (2, 1): 5}

        def where(self, index):
            ring, i = divmod(index, 6)
            part = i - 4 if i > 3 else i // 2
            step = (2, 2, 0, 1) if i > 3 else ((-1, 0, 1, 1), (1, 0, -1, -1))[i % 2]
            return ring, i, part, step[0]

        def go(self, index):
            ring, i, part, _ = self.where(index)
            up = 1 if i in (0, 2, 4) else -1
            moved = 0 if i < 4 else -up
            if ring == 0:
                a, b, device = moved, 0, self.dev1[up]
            else:
                a, b, device = self.OFF[ring - 1], moved, self.dev2[up]
            if i > 3:
                self.need(index - i + (0 if i == 4 else 3))
            elif ring > 1:
                self.need(self.CAME[(a, part)])
            elif a == 0 and moved == 0:
                self.slots(part)
            self.send(a, b, part, device, index)

        def slots(self, part):
            k = {(0, 0): 0, (0, 1): 3, (1, 0): 1, (1, 1): 2}[(self.half, part)]
            if k not in landed:
                landed.add(k)
                z_arrived(k)

        def need(self, index):
            if (self.half, index) in landed:
                return
            landed.add((self.half, index))
            ring, i, part, off = self.where(index)
            a, b = (off, 0) if ring == 0 else (self.OFF[ring - 1], off)
            self.arrived(a, b, part, index)

    def scaled(codes, scales):
        rows, cols = codes.shape
        blocks = codes.reshape(rows // 32, 32, cols) * scales[:, None, :]
        return blocks.reshape(rows, cols)

    def accumulate(xx, fresh):
        cols = pl.ds(mult(xx * wide, 128), wide)
        scale_rows = pl.ds(mult(xx * (wide // 32), 16), wide // 32)
        for s in range(2):
            for codes, scales, total in ((GC, GS, GACC), (UC, US, UACC)):
                value = jnp.dot(
                    X[:, cols], scaled(codes[s, cols, :], scales[s, scale_rows, :]),
                    preferred_element_type=F32,
                )
                total[s] = value if fresh else total[s] + value

    A, B = Gather(0, as_sem, ar_sem), Gather(1, bs_sem, br_sem)
    halves = (A, B)
    landed = set()
    def column(offset):
        low, high = {0: (None, None), 3: ((0, 2), 1), 1: ((1, 3), 2), 2: ((4, 5), 3)}[offset]
        if offset == 0:
            for i in range(6):
                A.need(i)
            B.slots(0)
            B.slots(1)
        else:
            for j in range(4):
                for i in low:
                    A.need(6 + 6 * j + i)
            for i in low:
                B.need(i)
        for i in range(6):
            B.need(6 + 6 * (high or 0) + i)

    fresh = True
    for kind, index in GATHER_ORDER:
        if kind < 2:
            halves[kind].go(index)
            continue
        if fresh:
            for copy in local_w:
                copy.wait()
            for copy in remote_w[:4]:
                copy.wait_recv()
        column(index)
        accumulate(xs[index], fresh)
        fresh = False
    for half in range(2):
        for index in range(30):
            halves[half].need(index)
    for copy in remote_w[4:]:
        copy.wait_recv()
    units = GACC.shape[2]
    for s in range(2):
        gate = GACC[s]
        hidden = gate / (1.0 + jnp.exp(-gate)) * UACC[s]
        H[:, s * units:(s + 1) * units] = hidden.astype(BF)

    def project(xx):
        piece = 512
        for i in range(wide // piece):
            cols = pl.ds(mult(xx * wide + i * piece, 128), piece)
            total = None
            for s in range(2):
                part = jnp.dot(
                    H[:, s * 256:(s + 1) * 256], scaled(DC[s, :, cols], DS[s, :, cols]),
                    preferred_element_type=F32,
                )
                total = part if total is None else total + part
            PS[:, cols] = total.astype(BF)

    class Reduce:
        def __init__(self, half, base, R1, R2):
            self.half, self.base, self.R1, self.R2 = half, base, R1, R2
            self.line = xs if half == 0 else ys
            self.other = ys if half == 0 else xs
            self.dev1 = dev_x if half == 0 else dev_y
            self.dev2 = dev_y if half == 0 else dev_x

        def reg(self, a, b, part):
            p, q = self.line[a % 4], self.other[b % 4]
            yy, xx = (q, p) if self.half == 0 else (p, q)
            return region(PS, self.half, yy, xx, part)

        def copy(self, src, dst, device, index):
            return pltpu.make_async_remote_copy(
                src_ref=src, dst_ref=dst, send_sem=rs_send.at[self.base + index],
                recv_sem=rs_recv.at[self.base + index], device_id=device, device_id_type=MESH,
            )

        def send(self, src, dst, device, index):
            copy = self.copy(src, dst, device, index)
            copy.start()
            sends.append(copy)

        def arrived(self, dst, index):
            self.copy(dst, dst, partner, index).wait_recv()

        def go(self, index):
            j, i = divmod(index, 4)
            pieces, buf, base = self.ring1(j) if j < 4 else (self.ring2, self.R2, 16)
            devices = self.dev1 if j < 4 else self.dev2
            down, part = i % 2 == 0, i % 2
            device = devices[-1 if down else 1]
            landing = buf.at[pl.ds(64 + 16 * part, 16)]
            if i < 2:
                self.send(pieces(2, part), landing, device, index)
                return
            a = -1 if down else 1
            self.arrived(landing, base + part)
            mine = pieces(a, part)
            mine[...] = (mine[...].astype(F32) + landing[...].astype(F32)).astype(BF)
            self.send(pieces(a, None), buf.at[pl.ds(32 if down else 0, 32)], device, index)

        def own(self, pieces, buf, index):
            self.arrived(buf.at[pl.ds(32, 32)], index + 2)
            self.arrived(buf.at[pl.ds(0, 32)], index + 3)
            total = pieces(0, None)[...].astype(F32) + buf[0:32, :].astype(F32)
            return (total + buf[32:64, :].astype(F32)).astype(BF)

        OFF = (2, 1, -1, 0)

        def ring1(self, j):
            return (lambda a, part: self.reg(a, self.OFF[j], part)), self.R1.at[j], 4 * j

        def own1(self, j):
            pieces, buf, index = self.ring1(j)
            value = self.own(pieces, buf, index)
            pieces(0, None)[...] = value

        def ring2(self, a, part):
            return self.reg(0, a, part)

        def own2(self):
            FIN[self.half * 32:(self.half + 1) * 32, :] = self.own(self.ring2, self.R2, 16)

    reduces = (Reduce(0, 0, RA, RA2), Reduce(1, 20, RB, RB2))

    returns = []

    def give_back(k):
        zt = lax.rem(z + 2 * k + odd, NZ)
        for cc in range(2):
            src = FIN.at[pl.ds({0: 0, 3: 16, 1: 32, 2: 48}[k], 16), pl.ds(cc * feat, feat)]
            dst = YB.at[pl.ds(mult(z * CAP, CAP), CAP), :]
            copy = pltpu.make_async_remote_copy(
                src_ref=src, dst_ref=dst, send_sem=fs_sem.at[k * 2 + cc], recv_sem=fr_sem.at[z],
                device_id=dev(zt, y, x, cc), device_id_type=MESH,
            )
            if k > 0:
                copy.start()
                returns.append((None, copy))
                continue
            here = jnp.logical_and(odd == 0, c == cc)
            pl.when(jnp.logical_not(here))(copy.start)
            returns.append((here, copy))

            @pl.when(here)
            def _():
                move = pltpu.make_async_copy(src, dst, zl_sem)
                move.start()
                move.wait()

    for kind, index in REDUCE_ORDER:
        if kind == 2:
            project(xs[index])
        elif index < 20:
            reduces[kind].go(index)
        elif index < 24:
            reduces[kind].own1(index - 20)
        else:
            reduces[kind].own2()
            for k in ((3, 0), (2, 1))[kind]:
                give_back(k)

    for copy in remote_w:
        copy.wait_send()
    for dz, copy in z_sends:
        if dz == 0:
            pl.when(jnp.logical_not(at_home))(copy.wait_send)
        else:
            copy.wait_send()
    for copy in sends:
        copy.wait_send()

    for e in range(EXPERTS):
        dst = YB.at[pl.ds(e * CAP, CAP), :]
        copy = pltpu.make_async_remote_copy(
            src_ref=dst, dst_ref=dst, send_sem=fs_sem.at[0], recv_sem=fr_sem.at[e],
            device_id=partner, device_id_type=MESH,
        )
        here = jnp.logical_and(z == e, at_home)
        pl.when(jnp.logical_not(here))(copy.wait_recv)

    mixed = jnp.dot(WHI[...], YB[...], preferred_element_type=F32)
    mixed = mixed + jnp.dot(WLO[...], YB[...], preferred_element_type=F32)
    out[...] = mixed.astype(BF)

    for here, copy in returns:
        if here is None:
            copy.wait_send()
        else:
            pl.when(jnp.logical_not(here))(copy.wait_send)


def per_device(tokens, ids, combine, gate_c, gate_s, up_c, up_s, down_c, down_s):
    count, feat = tokens.shape
    deep, units = gate_c.shape
    wide = 2 * feat
    vmem, hbm = pl.BlockSpec(memory_space=pltpu.VMEM), pl.BlockSpec(memory_space=pl.ANY)
    dma = pltpu.SemaphoreType.DMA
    return pl.pallas_call(
        kernel,
        out_shape=jax.ShapeDtypeStruct((count, feat), BF),
        in_specs=[hbm] * 9,
        out_specs=vmem,
        scratch_shapes=[
            pltpu.VMEM((count, feat), BF),
            pltpu.VMEM((2, count), jnp.int32),
            pltpu.VMEM((2, count), F32),
            pltpu.VMEM((2, 256, units), F32),
            pltpu.VMEM((2, 256, units), F32),
            pltpu.VMEM((EXPERTS * CAP, feat), BF),
            pltpu.VMEM((256, deep), BF),
            pltpu.VMEM((256, deep), BF),
            pltpu.VMEM((256, 2 * units), BF),
            pltpu.VMEM((64, wide), BF),
            pltpu.VMEM((EXPERTS * CAP, feat), BF),
            pltpu.VMEM((EXPERTS * CAP, count), F32),
            pltpu.VMEM((count, EXPERTS * CAP), BF),
            pltpu.VMEM((count, EXPERTS * CAP), BF),
            pltpu.VMEM((4, 96, wide), BF),
            pltpu.VMEM((4, 96, wide), BF),
            pltpu.VMEM((96, wide), BF),
            pltpu.VMEM((96, wide), BF),
            pltpu.VMEM((2,) + gate_c.shape, BF),
            pltpu.VMEM((2,) + gate_s.shape, BF),
            pltpu.VMEM((2,) + up_c.shape, BF),
            pltpu.VMEM((2,) + up_s.shape, BF),
            pltpu.VMEM((2,) + down_c.shape, BF),
            pltpu.VMEM((2,) + down_s.shape, BF),
            dma((3,)), dma((6,)), dma((6,)), dma((6,)), dma((8,)), dma((8,)), dma,
            dma((30,)), dma((30,)), dma((30,)), dma((30,)),
            dma((40,)), dma((40,)), dma((8,)), dma((8,)),
        ],
        compiler_params=pltpu.CompilerParams(
            collective_id=0, has_side_effects=True, vmem_limit_bytes=63 * 2**20
        ),
        name="moe",
    )(tokens, jnp.transpose(ids), jnp.transpose(combine), gate_c, gate_s, up_c, up_s, down_c, down_s)


def solution(mesh):
    placed = (
        P("ep", "tp"),
        P("ep", None),
        P("ep", None),
        P(None, ("ep", "tp")),
        P(None, ("ep", "tp")),
        P(None, ("ep", "tp")),
        P(None, ("ep", "tp")),
        P(("ep", "tp"), None),
        P(("ep", "tp"), None),
    )
    return jax.shard_map(
        per_device, mesh=mesh, in_specs=placed, out_specs=P("ep", "tp"), check_vma=False
    )
```
